32 devices in a mesh: hist: 8 (over z, y), second: 4 (over x, core).
Axes of the slice: x: 2, y: 2, z: 4, core: 2. Of those that a mesh axis runs over, the one named last changes fastest.
Arguments:
- history: bfloat16 [32, 64, 32, 2, 128], P('hist', None, 'second'), may hold values from -0.29882812 to 0.29882812
- row_now: float32 [64, 32, 256], P('hist', 'second'), may hold values from -4.2 to 4.2
- coupling: float32 [64, 64], P('hist'), may hold values from 0.5 to 1.5
- step_inverse: float32 [3, 2, 64, 64], replicated, may hold values from -0.5 to 0.5
- start_step: int32 [1], replicated, may hold values from 16 to 28
- history_time: int32 [32], P('hist'), may hold values from 0 to 31, each once
Outputs:
- green_next: float32 [64, 32, 256], P('hist', 'second')
The draws below stay inside these ranges and needn't reach their ends.
Inputs may be any that keep to these rules, and one draw needn't show every extreme that they name: history_time holds every time from 0 to 31 once.
All inputs are finite; a program needn't handle non-finite values.
Results may differ from the reference program's by a relative error of at most 0.011.
Values may be sent and summed in bfloat16 or wider, within the bound.
No kernel may reach another device: no remote copies, remote signals or barrier semaphores. Data moves between devices by JAX's collectives and lax.ppermute only.
A program may use at most 64 MiB of HBM per device.

```python
import math
import jax
import jax.numpy as jnp
from jax import lax

ORBITALS = 64
SLOTS_DEV = 4
STEPS = 3
TIMES = 32
N_HIST = 8


def strengthened(drawn, rng, source, target, parts, factor):
    def block_of(dim):
        return (jnp.arange(drawn.shape[dim]) // (drawn.shape[dim] // parts)).reshape((-1,) + (1,) * (drawn.ndim - 1 - dim))

    first = jax.random.permutation(rng, parts)[block_of(target)]
    second = (block_of(target) + parts // 2) % parts
    return jnp.where((block_of(source) == first) | (block_of(source) == second), factor * drawn, drawn)


def steps_of(key, dims, shards, least, high):
    loudness = 1.0
    for dim, blocks in shards:
        draws = jax.random.uniform(jax.random.fold_in(jax.random.fold_in(key, 6), dim), (blocks,), jnp.float32, least / len(shards), high / len(shards))
        loudness = loudness * jnp.repeat(jnp.exp(draws), dims[dim] // blocks).reshape((-1,) + (1,) * (len(dims) - 1 - dim))
    return loudness


def bell_draw(stream_key, extent, deviation, reach, cuts=(), kind=jnp.bfloat16):
    array = jax.random.normal(stream_key, extent, jnp.float32) * deviation
    if len(cuts) > 0:
        array = steps_of(stream_key, extent, cuts, -0.22, 0.18) * array
    return jnp.clip(array, min=-reach, max=reach).astype(kind)


def bell_draw_with(key, shape, width, limit, shards, heavy, held_as=jnp.bfloat16):
    result = width * jax.random.normal(key, shape, jnp.float32)
    if shards:
        result = result * steps_of(key, shape, shards, -0.22, 0.18)
    return jnp.clip(strengthened(result, jax.random.fold_in(key, 3), *heavy), -limit, limit).astype(held_as)


def setup_inputs(seed: int = 0) -> dict:
    keys = jax.random.split(jax.random.key(seed), 7)
    return {
        "history": bell_draw_with(keys[0], (TIMES, ORBITALS, TIMES, 2, 2 * ORBITALS), 0.05, 0.29882812, ((0, 8), (2, 4)), (0, 4, 8, 2.0)),
        "row_now": bell_draw(keys[1], (ORBITALS, TIMES, 4 * ORBITALS), 0.7, 4.2, ((0, 8), (1, 4)), jnp.float32),
        "coupling": jnp.clip(jnp.exp(math.log(1.5) - 1.0986123 * jax.random.uniform(keys[2], (ORBITALS, ORBITALS), jnp.float32) ** steps_of(keys[2], (ORBITALS, ORBITALS), ((0, 8),), -0.2, 0.2)), 0.5, 1.5),
        "step_inverse": bell_draw(keys[3], (STEPS, 2, ORBITALS, ORBITALS), (2 * ORBITALS) ** -0.5, 0.5, (), jnp.float32),
        "start_step": jax.random.randint(keys[4], (1,), TIMES // 2, TIMES - 3).astype(jnp.int32),
        "history_time": jax.random.permutation(keys[5], TIMES).astype(jnp.int32),
    }


step_width = 0.05
highest = lax.Precision.HIGHEST


def cubic_term(first_real, first_imag, other_real, other_imag):
    square_real = first_real * first_real - first_imag * first_imag
    square_imag = 2.0 * first_real * first_imag
    return (square_real * other_real + square_imag * other_imag,
            square_imag * other_real - square_real * other_imag)


def self_energy(green_row, coupling):
    weight_sq = (coupling * coupling)[:, None, :]
    lesser_real, lesser_imag = green_row[:, :, 0, 0], green_row[:, :, 0, 1]
    greater_real, greater_imag = green_row[:, :, 1, 0], green_row[:, :, 1, 1]
    less_real, less_imag = cubic_term(lesser_real, lesser_imag, greater_real, greater_imag)
    more_real, more_imag = cubic_term(greater_real, greater_imag, lesser_real, lesser_imag)
    diff_real = weight_sq * (more_real - less_real)
    diff_imag = weight_sq * (more_imag - less_imag)
    stacked = jnp.stack([diff_real, diff_imag], axis=2)
    return stacked.reshape(green_row.shape[0], green_row.shape[1], 2 * green_row.shape[4]).astype(jnp.bfloat16)


def advance(green_row, summed, inverse_pair):
    real_sum = summed[:, :, :, 0, 0, :] - summed[:, :, :, 1, 1, :]
    imag_sum = summed[:, :, :, 1, 0, :] + summed[:, :, :, 0, 1, :]
    moved_real = green_row[:, :, :, 0, :] + step_width * real_sum
    moved_imag = green_row[:, :, :, 1, :] + step_width * imag_sum
    inverse_real = inverse_pair[0]
    inverse_imag = inverse_pair[1]
    new_real = (jnp.einsum("xa,btma->btmx", inverse_real, moved_real, precision=highest)
                - jnp.einsum("xa,btma->btmx", inverse_imag, moved_imag, precision=highest))
    new_imag = (jnp.einsum("xa,btma->btmx", inverse_real, moved_imag, precision=highest)
                + jnp.einsum("xa,btma->btmx", inverse_imag, moved_real, precision=highest))
    return jnp.stack([new_real, new_imag], axis=3)


def reference(history, row_now, coupling, step_inverse, start_step, history_time):
    anchor = start_step[0]
    alive_slot = history_time <= anchor
    green_row = row_now.reshape(ORBITALS, TIMES, 2, 2, ORBITALS)
    earlier = []
    for window_step in range(STEPS):
        energy = self_energy(green_row, coupling)
        energy_left = energy.reshape(ORBITALS, TIMES, 2, ORBITALS)
        selected = jnp.take(energy_left, history_time, axis=1)
        selected = jnp.where(alive_slot[None, :, None, None], selected, jnp.zeros((), jnp.bfloat16))

        def add_block(block_index, running):
            first_slot = (block_index * SLOTS_DEV).astype(jnp.int32)
            history_block = lax.dynamic_slice_in_dim(history, first_slot, SLOTS_DEV, 0).astype(jnp.float32)
            history_block = history_block.reshape(SLOTS_DEV, ORBITALS, TIMES, 2, ORBITALS, 2)
            left_rows = lax.dynamic_slice_in_dim(selected, first_slot, SLOTS_DEV, 1).astype(jnp.float32)
            return running + jnp.einsum("jsqa,sjtmbp->btmpqa", left_rows, history_block)

        summed = lax.fori_loop(0, N_HIST, add_block,
                               jnp.zeros((ORBITALS, TIMES, 2, 2, 2, ORBITALS), jnp.float32))
        for past_index, past_row in enumerate(earlier):
            column = lax.dynamic_index_in_dim(energy_left, (anchor + 1 + past_index).astype(jnp.int32), 1,
                                              keepdims=False).astype(jnp.float32)
            summed = summed + jnp.einsum("jqa,btmpj->btmpqa", column, past_row, precision=highest)
        green_row = advance(green_row, summed, step_inverse[window_step])
        earlier.append(green_row)
    return green_row.reshape(ORBITALS, TIMES, 4 * ORBITALS)
```

```python
import functools

import jax
import jax.numpy as jnp
from jax import lax
from jax.experimental import pallas as pl
from jax.experimental.pallas import tpu as pltpu
from jax.sharding import Mesh, PartitionSpec as P

step_width = 0.05
highest = lax.Precision.HIGHEST
bf16 = jnp.bfloat16
f32 = jnp.float32
vmem = pl.BlockSpec(memory_space=pltpu.VMEM)
smem = pl.BlockSpec(memory_space=pltpu.SMEM)


def pack_kernel(groups, peers, hist_ref, out_ref, wide_ref):
    rows = hist_ref.shape[0] // groups
    width = hist_ref.shape[1] // peers
    wide_ref[...] = hist_ref[...].astype(f32)
    for group in range(groups):
        turned = wide_ref[pl.ds(group, rows, stride=groups), :].T.astype(bf16)
        for peer in range(peers):
            out_ref[peer, group * width : (group + 1) * width, :] = turned[
                peer * width : (peer + 1) * width
            ]


def cubic_term(first_real, first_imag, other_real, other_imag):
    square_real = first_real * first_real - first_imag * first_imag
    square_imag = 2.0 * first_real * first_imag
    return (
        square_real * other_real + square_imag * other_imag,
        square_imag * other_real - square_real * other_imag,
    )


def energy_of(lesser, greater, weight_sq):
    half = lesser.shape[-1] // 2
    lr, li = lesser[:, :half], lesser[:, half:]
    gr, gi = greater[:, :half], greater[:, half:]
    less_real, less_imag = cubic_term(lr, li, gr, gi)
    more_real, more_imag = cubic_term(gr, gi, lr, li)
    return jnp.concatenate(
        [weight_sq * (more_real - less_real), weight_sq * (more_imag - less_imag)], axis=-1
    )


def send_energy(row_ref, coupling_ref, scratch_ref, send_ref):
    own_rows, slab, lanes = row_ref.shape
    for b in range(own_rows):
        row = row_ref[b]
        weight = coupling_ref[b : b + 1, :]
        scratch_ref[pl.ds(b, slab, stride=own_rows), :] = energy_of(
            row[:, : lanes // 2], row[:, lanes // 2 :], weight * weight
        )
    narrow = scratch_ref[...].astype(bf16)
    for peer in range(send_ref.shape[0]):
        send_ref[peer, : own_rows * slab, :] = narrow


def first_kernel(row_ref, coupling_ref, time_ref, send_ref, scratch_ref):
    own_rows, slab, lanes = row_ref.shape
    send_energy(row_ref, coupling_ref, scratch_ref, send_ref)
    pad = send_ref.shape[1] - own_rows * slab
    lane = lax.broadcasted_iota(jnp.int32, (pad, lanes // 2), 1)
    times = jnp.zeros((pad, lanes // 2), jnp.int32)
    for slot in range(time_ref.shape[0]):
        times = jnp.where(lane == slot, time_ref[slot], times)
    times = times.astype(f32).astype(bf16)
    for peer in range(send_ref.shape[0]):
        send_ref[peer, own_rows * slab :, :] = times


def step_kernel(
    n_past, last, time_ref, anchor_ref, core_ref, hist_ref, own_ref, other_ref, row_ref, *rest
):
    past_refs = rest[:n_past]
    inverse_ref, coupling_ref, out_ref = rest[n_past : n_past + 3]
    rest = rest[n_past + 3 :]
    if last:
        chosen_ref, sum_ref = rest
        send_ref = energy_ref = None
    else:
        send_ref, chosen_ref, sum_ref, energy_ref = rest
    peers, slab, own_rows = own_ref.shape[0], own_ref.shape[2], own_ref.shape[3]
    orbitals = peers * own_rows
    lanes = own_ref.shape[4]
    half = lanes // 2
    slots = time_ref.shape[0]
    block = slots // peers
    anchor = anchor_ref[0]
    core = core_ref[0]

    def energy_at(time):
        inner = lax.rem(time, slab)
        group = lax.div(time, slab)
        far = lax.div(group, 2)
        same = lax.rem(group, 2) == core
        return [
            jnp.where(same, own_ref[peer, far, inner], other_ref[peer, far, inner])
            for peer in range(peers)
        ]

    def choose(slot, carry):
        time = time_ref[slot]
        alive = time <= anchor
        for peer, part in enumerate(energy_at(time)):
            chosen_ref[slot, peer * own_rows : (peer + 1) * own_rows, :] = jnp.where(
                alive, part, jnp.zeros_like(part)
            )
        return carry

    lax.fori_loop(0, slots, choose, 0, unroll=slots <= 32)
    total = None
    for peer in range(peers):
        part = jnp.dot(
            hist_ref[peer],
            chosen_ref[peer * block : (peer + 1) * block].reshape(block * orbitals, lanes),
            preferred_element_type=f32,
        )
        total = part if total is None else total + part
    sum_ref[...] = total
    sign = jnp.where(lax.broadcasted_iota(jnp.int32, (1, lanes), 1) < half, -1.0, 1.0)
    columns = []
    for past in range(n_past):
        for peer, part in enumerate(energy_at(anchor + 1 + past)):
            chosen_ref[past, peer * own_rows : (peer + 1) * own_rows, :] = part
        columns.append(chosen_ref[past])
    for m in range(2):
        evens, odds = [], []
        for b in range(own_rows):
            first = m * 2 * own_rows + 2 * b
            evens.append(sum_ref[pl.ds(first, slab, stride=4 * own_rows), :])
            odds.append(sum_ref[pl.ds(first + 1, slab, stride=4 * own_rows), :])
        even = jnp.concatenate(evens, axis=0)
        odd = jnp.concatenate(odds, axis=0)
        for past_ref, column in zip(past_refs, columns):
            for part in range(2):
                start = m * lanes + part * half
                row = past_ref[:, :, start : start + half].reshape(own_rows * slab, half)
                high = row.astype(bf16)
                low = (row - high.astype(f32)).astype(bf16)
                product = jnp.dot(high, column, preferred_element_type=f32) + jnp.dot(
                    low, column, preferred_element_type=f32
                )
                if part == 0:
                    even = even + product
                else:
                    odd = odd + product
        integral = even + sign * pltpu.roll(odd, half, 1)
        row = row_ref[:, :, m * lanes : (m + 1) * lanes].reshape(own_rows * slab, lanes)
        moved = row + step_width * integral
        moved = lax.dot_general(
            moved, inverse_ref[...], (((1,), (1,)), ((), ())), precision=highest,
            preferred_element_type=f32,
        )
        out_ref[:, :, m * lanes : (m + 1) * lanes] = moved.reshape(own_rows, slab, lanes)
    if not last:
        send_energy(out_ref, coupling_ref, energy_ref, send_ref)


def body(history, row_now, coupling, step_inverse, start_step, history_time):
    slots_dev, orbitals, slab, parts, lanes = history.shape
    own_rows = row_now.shape[0]
    steps = step_inverse.shape[0]
    peers = lax.axis_size("hist")
    far = lax.axis_size("x")
    groups = slab * parts
    width = lanes // peers
    n_sum = groups * width
    shape = jax.ShapeDtypeStruct
    packed = pl.pallas_call(
        functools.partial(pack_kernel, groups, peers),
        out_shape=shape((peers, n_sum, slots_dev * orbitals), bf16),
        in_specs=[vmem],
        out_specs=vmem,
        scratch_shapes=[pltpu.VMEM((slots_dev * orbitals * groups, lanes), f32)],
        name="pack",
    )(history.reshape(slots_dev * orbitals * groups, lanes))
    local = lax.all_to_all(packed, "hist", split_axis=0, concat_axis=0, tiled=True)
    pad = 16
    rows = slab * own_rows
    sent = pl.pallas_call(
        first_kernel,
        out_shape=shape((peers * far, rows + pad, lanes), bf16),
        in_specs=[vmem, vmem, smem],
        out_specs=vmem,
        scratch_shapes=[pltpu.VMEM((rows, lanes), f32)],
        name="first",
    )(row_now, coupling, history_time)
    real, imag = step_inverse[:, 0], step_inverse[:, 1]
    inverse = jnp.concatenate(
        [jnp.concatenate([real, -imag], axis=2), jnp.concatenate([imag, real], axis=2)], axis=1
    )
    core = lax.axis_index("c").reshape(1)
    green, past = row_now, []
    times = None
    for w in range(steps):
        last = w == steps - 1
        own = lax.all_to_all(sent, ("hist", "x"), split_axis=0, concat_axis=0, tiled=True)
        if w == 0:
            times = own.reshape(peers, far, rows + pad, lanes)[:, 0, rows, :slots_dev]
            times = times.astype(jnp.int32).reshape(peers * slots_dev)
            own = own[:, :rows]
        other = lax.ppermute(own, "c", [(0, 1), (1, 0)])
        split = (peers, far, slab, own_rows, lanes)
        outs = [shape(row_now.shape, f32)]
        scratch = [
            pltpu.VMEM((peers * slots_dev, orbitals, lanes), bf16),
            pltpu.VMEM((n_sum, lanes), f32),
        ]
        if not last:
            outs.append(shape((peers * far, rows, lanes), bf16))
            scratch.append(pltpu.VMEM((rows, lanes), f32))
        result = pl.pallas_call(
            functools.partial(step_kernel, len(past), last),
            out_shape=outs,
            in_specs=[smem] * 3 + [vmem] * (6 + len(past)),
            out_specs=[vmem] * len(outs),
            scratch_shapes=scratch,
            name=f"step{w}",
        )(
            times,
            start_step,
            core,
            local,
            own.reshape(split),
            other.reshape(split),
            green,
            *past,
            inverse[w],
            coupling,
        )
        green = result[0]
        if not last:
            sent = result[1]
            past.append(green)
    return green


def solution(mesh):
    n_hist, n_second = mesh.devices.shape
    split = Mesh(mesh.devices.reshape(n_hist, n_second // 2, 2), ("hist", "x", "c"))
    second = ("x", "c")
    placed = (
        P("hist", None, second, None, None),
        P("hist", second, None),
        P("hist", None),
        P(),
        P(),
        P("hist"),
    )
    return jax.shard_map(
        body, mesh=split, in_specs=placed, out_specs=P("hist", second, None), check_vma=False
    )
```

```python
import functools

import jax
import jax.numpy as jnp
from jax import lax
from jax.experimental import pallas as pl
from jax.experimental.pallas import tpu as pltpu
from jax.sharding import Mesh, PartitionSpec as P


step_width = 0.05
highest = lax.Precision.HIGHEST
bf16 = jnp.bfloat16
f32 = jnp.float32
vmem = pl.BlockSpec(memory_space=pltpu.VMEM)
smem = pl.BlockSpec(memory_space=pltpu.SMEM)
params = pltpu.CompilerParams(vmem_limit_bytes=16 * 2**20)


def local(x):
    return pltpu.with_memory_space_constraint(x, pltpu.VMEM)


def pack_kernel(groups, place_ref, hist_ref, *rest):
    out_refs, (wide_ref, turned_ref) = rest[:-2], rest[-2:]
    rows = hist_ref.shape[0] // groups
    width = hist_ref.shape[1] // len(out_refs)
    wide_ref[...] = hist_ref[...].astype(f32)
    for group in range(groups):
        turned = wide_ref[pl.ds(group, rows, stride=groups), :].T
        for peer in range(len(out_refs)):
            turned_ref[group % 2, peer] = turned[peer * width : (peer + 1) * width]
        for offset, out_ref in enumerate(out_refs):
            out_ref[group * width : (group + 1) * width, :] = turned_ref[
                group % 2, place_ref[0] ^ offset
            ].astype(bf16)


def cubic_term(first_real, first_imag, other_real, other_imag):
    square_real = first_real * first_real - first_imag * first_imag
    square_imag = 2.0 * first_real * first_imag
    return (
        square_real * other_real + square_imag * other_imag,
        square_imag * other_real - square_real * other_imag,
    )


def energy_of(lesser, greater, weight_sq):
    half = lesser.shape[-1] // 2
    lr, li = lesser[:, :half], lesser[:, half:]
    gr, gi = greater[:, :half], greater[:, half:]
    less_real, less_imag = cubic_term(lr, li, gr, gi)
    more_real, more_imag = cubic_term(gr, gi, lr, li)
    return jnp.concatenate(
        [weight_sq * (more_real - less_real), weight_sq * (more_imag - less_imag)], axis=-1
    )


def send_energy(row_ref, coupling_ref, scratch_ref, send_ref):
    own_rows, slab, lanes = row_ref.shape
    for b in range(own_rows):
        row = row_ref[b]
        weight = coupling_ref[b : b + 1, :]
        scratch_ref[pl.ds(b, slab, stride=own_rows), :] = energy_of(
            row[:, : lanes // 2], row[:, lanes // 2 :], weight * weight
        )
    for t in range(slab):
        narrow = scratch_ref[t * own_rows : (t + 1) * own_rows, :].astype(bf16)
        for peer in range(send_ref.shape[0]):
            send_ref[peer, t] = narrow


def first_kernel(row_ref, coupling_ref, time_ref, send_ref, scratch_ref):
    slab, own_rows, lanes = row_ref.shape[1], row_ref.shape[0], send_ref.shape[3]
    send_energy(row_ref, coupling_ref, scratch_ref, send_ref)
    lane = lax.broadcasted_iota(jnp.int32, (own_rows, lanes), 1)
    times = jnp.zeros((own_rows, lanes), jnp.int32)
    for slot in range(time_ref.shape[0]):
        times = jnp.where(lane == slot, time_ref[slot], times)
    narrow = times.astype(f32).astype(bf16)
    for peer in range(send_ref.shape[0]):
        send_ref[peer, slab] = narrow


def prepare_kernel(row_ref, high_ref, low_ref):
    row = row_ref[...]
    high = row.astype(bf16)
    high_ref[...] = high
    low_ref[...] = (row - high.astype(f32)).astype(bf16)


def step_kernel(
    peers, n_past, relative, last, time_ref, anchor_ref, place_ref, own_ref, other_ref, row_ref, *rest
):
    hist_refs, rest = rest[:peers], rest[peers:]
    past_refs = rest[: 2 * n_past]
    inverse_ref, coupling_ref, out_ref = rest[2 * n_past : 2 * n_past + 3]
    rest = rest[2 * n_past + 3 :]
    if last:
        chosen_ref, sum_ref = rest
        send_ref = energy_ref = None
    else:
        send_ref, chosen_ref, sum_ref, energy_ref = rest
    own_rows, lanes = own_ref.shape[3], own_ref.shape[4]
    slab = row_ref.shape[1]
    orbitals = peers * own_rows
    half = lanes // 2
    slots = time_ref.shape[0]
    block = slots // peers
    anchor = anchor_ref[0]
    hist_place, far_place, core = place_ref[0], place_ref[1], place_ref[2]

    def energy_at(time):
        inner = lax.rem(time, slab)
        group = lax.div(time, slab)
        far = lax.div(group, 2)
        same = lax.rem(group, 2) == core
        parts = []
        for peer in range(peers):
            place = far ^ far_place if relative else far
            parts.append(jnp.where(same, own_ref[peer, place, inner], other_ref[peer, place, inner]))
        return parts

    def choose(source, slot):
        time = time_ref[(source ^ hist_place) * block + slot]
        alive = time <= anchor
        for peer, part in enumerate(energy_at(time)):
            chosen_ref[source * block + slot, peer * own_rows : (peer + 1) * own_rows, :] = (
                jnp.where(alive, part, jnp.zeros_like(part))
            )

    if slots <= 32:
        for source in range(peers):
            for slot in range(block):
                choose(source, slot)
    else:

        @pl.loop(0, peers)
        def _(source):
            for slot in range(block):
                choose(source, slot)

    total = None
    for peer in range(peers):
        part = jnp.dot(
            hist_refs[peer][...],
            chosen_ref[peer * block : (peer + 1) * block].reshape(block * orbitals, lanes),
            preferred_element_type=f32,
        )
        total = part if total is None else total + part
    sum_ref[...] = total
    sign = jnp.where(lax.broadcasted_iota(jnp.int32, (1, lanes), 1) < half, -1.0, 1.0)
    columns = []
    for past in range(n_past):
        for peer, part in enumerate(energy_at(anchor + 1 + past)):
            chosen_ref[past, peer * own_rows : (peer + 1) * own_rows, :] = part
        columns.append(chosen_ref[past])
    for m in range(2):
        evens, odds = [], []
        for b in range(own_rows):
            first = m * 2 * own_rows + 2 * b
            evens.append(sum_ref[pl.ds(first, slab, stride=4 * own_rows), :])
            odds.append(sum_ref[pl.ds(first + 1, slab, stride=4 * own_rows), :])
        even = jnp.concatenate(evens, axis=0)
        odd = jnp.concatenate(odds, axis=0)
        for past, column in enumerate(columns):
            for past_ref in past_refs[2 * past : 2 * past + 2]:
                start = m * lanes
                even += jnp.dot(
                    past_ref[:, start : start + half], column, preferred_element_type=f32
                )
                odd += jnp.dot(
                    past_ref[:, start + half : start + lanes], column, preferred_element_type=f32
                )
        integral = even + sign * pltpu.roll(odd, half, 1)
        row = row_ref[:, :, m * lanes : (m + 1) * lanes].reshape(own_rows * slab, lanes)
        moved = lax.dot_general(
            row + step_width * integral,
            inverse_ref[...],
            (((1,), (1,)), ((), ())),
            precision=highest,
            preferred_element_type=f32,
        )
        out_ref[:, :, m * lanes : (m + 1) * lanes] = moved.reshape(own_rows, slab, lanes)
    if not last:
        send_energy(out_ref, coupling_ref, energy_ref, send_ref)


def spread(block, axis):
    size = lax.axis_size(axis)
    gathered = block[None]
    stride = size // 2
    while stride:
        ring = [(i, i ^ stride) for i in range(size)]
        other = lax.ppermute(gathered, axis, ring)
        gathered = jnp.stack([gathered, other], axis=1).reshape(-1, *block.shape)
        stride //= 2
    return gathered


def body(history, row_now, coupling, step_inverse, start_step, history_time):
    slots_dev, orbitals, slab, parts, lanes = history.shape
    own_rows = row_now.shape[0]
    steps = step_inverse.shape[0]
    peers = lax.axis_size("hist")
    far = lax.axis_size("x")
    groups = slab * parts
    width = lanes // peers
    n_sum = groups * width
    rows = slab * own_rows
    place = jnp.stack([lax.axis_index(name) for name in ("hist", "x", "c")])
    packed = pl.pallas_call(
        functools.partial(pack_kernel, groups),
        out_shape=[pltpu.VMEM((n_sum, slots_dev * orbitals), bf16)] * peers,
        in_specs=[smem, vmem],
        out_specs=[vmem] * peers,
        scratch_shapes=[
            pltpu.VMEM((slots_dev * orbitals * groups, lanes), f32),
            pltpu.VMEM((2, peers, width, slots_dev * orbitals), f32),
        ],
        compiler_params=params,
        name="pack",
    )(place, history.reshape(slots_dev * orbitals * groups, lanes))
    sent = pl.pallas_call(
        first_kernel,
        out_shape=pltpu.VMEM((peers, slab + 1, own_rows, lanes), bf16),
        in_specs=[vmem, vmem, smem],
        out_specs=vmem,
        scratch_shapes=[pltpu.VMEM((rows, lanes), f32)],
        compiler_params=params,
        name="first",
    )(row_now, coupling, history_time)
    moved = [packed[0]]
    for offset in range(1, peers):
        ring = [(i, i ^ offset) for i in range(peers)]
        moved.append(lax.ppermute(packed[offset], "hist", ring))
    real, imag = step_inverse[:, 0], step_inverse[:, 1]
    inverse = jnp.concatenate(
        [jnp.concatenate([real, -imag], axis=2), jnp.concatenate([imag, real], axis=2)], axis=1
    )
    green, past = row_now, []
    times = None
    for w in range(steps):
        last = w == steps - 1
        if w == 0:
            own = lax.all_to_all(sent, "hist", split_axis=0, concat_axis=0, tiled=True)
            times = own[:, slab, 0, :slots_dev].astype(jnp.int32).reshape(peers * slots_dev)
            own = spread(own, "x").swapaxes(0, 1)
        else:
            own = lax.all_to_all(sent, ("hist", "x"), split_axis=0, concat_axis=0, tiled=True)
            own = own.reshape(peers, far, slab, own_rows, lanes)
            past += pl.pallas_call(
                prepare_kernel,
                out_shape=[pltpu.VMEM((rows, 2 * lanes), bf16)] * 2,
                in_specs=[vmem],
                out_specs=[vmem] * 2,
                compiler_params=params,
            )(local(green.reshape(rows, 2 * lanes)))
        other = lax.ppermute(own, "c", [(0, 1), (1, 0)])
        scratch = [
            pltpu.VMEM((peers * slots_dev, orbitals, lanes), bf16),
            pltpu.VMEM((n_sum, lanes), f32),
        ]
        if last:
            outs = [jax.ShapeDtypeStruct(row_now.shape, f32)]
        else:
            outs = [
                pltpu.VMEM(row_now.shape, f32),
                pltpu.VMEM((peers * far, slab, own_rows, lanes), bf16),
            ]
            scratch.append(pltpu.VMEM((rows, lanes), f32))
        result = pl.pallas_call(
            functools.partial(step_kernel, peers, len(past) // 2, w == 0, last),
            out_shape=outs,
            in_specs=[smem] * 3 + [vmem] * (5 + peers + len(past)),
            out_specs=[vmem] * len(outs),
            scratch_shapes=scratch,
            compiler_params=params,
        )(
            times,
            start_step,
            place,
            local(own),
            local(other),
            local(green),
            *[local(block) for block in moved],
            *[local(row) for row in past],
            local(inverse[w]),
            local(coupling),
        )
        green = result[0]
        if not last:
            sent = result[1]
    return green


def solution(mesh):
    n_hist, n_second = mesh.devices.shape
    split = Mesh(mesh.devices.reshape(n_hist, n_second // 2, 2), ("hist", "x", "c"))
    second = ("x", "c")
    placed = (
        P("hist", None, second, None, None),
        P("hist", second, None),
        P("hist", None),
        P(),
        P(),
        P("hist"),
    )
    return jax.shard_map(
        body, mesh=split, in_specs=placed, out_specs=P("hist", second, None), check_vma=False
    )
```

```python
import functools

import jax
import jax.numpy as jnp
from jax import lax
from jax.experimental import pallas as pl
from jax.experimental.pallas import tpu as pltpu
from jax.sharding import Mesh, PartitionSpec as P


step_width = 0.05
highest = lax.Precision.HIGHEST
bf16 = jnp.bfloat16
f32 = jnp.float32
vmem = pl.BlockSpec(memory_space=pltpu.VMEM)
smem = pl.BlockSpec(memory_space=pltpu.SMEM)
hbm = pl.BlockSpec(memory_space=pltpu.HBM)
params = pltpu.CompilerParams(vmem_limit_bytes=32 * 2**20)


def local(x):
    return pltpu.with_memory_space_constraint(x, pltpu.VMEM)


def remote(x):
    return pltpu.with_memory_space_constraint(x, pltpu.HBM)


def pack_kernel(groups, place_ref, hist_hbm, *rest):
    out_refs, (hist_ref, wide_ref, turned_ref, sems) = rest[:-4], rest[-4:]
    rows = 128 * groups
    width = hist_ref.shape[1] // len(out_refs)
    half = width // 2
    chunks = [pl.ds(c * rows, rows) for c in range(hist_ref.shape[0] // rows)]
    copies = [
        pltpu.make_async_copy(hist_hbm.at[chunk], hist_ref.at[chunk], sems.at[c])
        for c, chunk in enumerate(chunks)
    ]
    for copy in copies:
        copy.start()
    for c, copy in enumerate(copies):
        copy.wait()
        wide_ref[chunks[c], :] = hist_ref[chunks[c], :].astype(f32)
        columns = slice(c * 128, (c + 1) * 128)
        for group in range(groups):
            turned = wide_ref[pl.ds(c * rows + group, 128, stride=groups), :].T
            for peer in range(len(out_refs)):
                turned_ref[group % 2, peer] = turned[peer * width : (peer + 1) * width]
            for offset, out_ref in enumerate(out_refs):
                for part in range(2):
                    start = (part * groups + group) * half
                    out_ref[start : start + half, columns] = turned_ref[
                        group % 2, place_ref[0] ^ offset, pl.ds(part, half, stride=2), :
                    ].astype(bf16)


def cubic_term(first_real, first_imag, other_real, other_imag):
    square_real = first_real * first_real - first_imag * first_imag
    square_imag = 2.0 * first_real * first_imag
    return (
        square_real * other_real + square_imag * other_imag,
        square_imag * other_real - square_real * other_imag,
    )


def energy_of(lesser, greater, weight_sq):
    half = lesser.shape[-1] // 2
    lr, li = lesser[:, :half], lesser[:, half:]
    gr, gi = greater[:, :half], greater[:, half:]
    less_real, less_imag = cubic_term(lr, li, gr, gi)
    more_real, more_imag = cubic_term(gr, gi, lr, li)
    return jnp.concatenate(
        [weight_sq * (more_real - less_real), weight_sq * (more_imag - less_imag)], axis=-1
    )


def send_energy(row_ref, coupling_ref, scratch_ref, send_ref):
    own_rows, slab, lanes = row_ref.shape
    for b in range(own_rows):
        row = row_ref[b]
        weight = coupling_ref[b : b + 1, :]
        scratch_ref[pl.ds(b, slab, stride=own_rows), :] = energy_of(
            row[:, : lanes // 2], row[:, lanes // 2 :], weight * weight
        )
    for t in range(slab):
        narrow = scratch_ref[t * own_rows : (t + 1) * own_rows, :].astype(bf16)
        for peer in range(send_ref.shape[0]):
            send_ref[peer, t] = narrow


def first_kernel(row_hbm, coupling_hbm, time_hbm, send_ref, row_ref, coupling_ref, time_ref, scratch_ref, sems):
    pairs = ((row_hbm, row_ref), (coupling_hbm, coupling_ref), (time_hbm, time_ref))
    copies = [pltpu.make_async_copy(a, b, sems.at[i]) for i, (a, b) in enumerate(pairs)]
    for copy in copies:
        copy.start()
    for copy in copies:
        copy.wait()
    slab, own_rows, lanes = row_ref.shape[1], row_ref.shape[0], send_ref.shape[3]
    send_energy(row_ref, coupling_ref, scratch_ref, send_ref)
    lane = lax.broadcasted_iota(jnp.int32, (own_rows, lanes), 1)
    times = jnp.zeros((own_rows, lanes), jnp.int32)
    for slot in range(time_ref.shape[0]):
        times = jnp.where(lane == slot, time_ref[slot], times)
    narrow = times.astype(f32).astype(bf16)
    for peer in range(send_ref.shape[0]):
        send_ref[peer, slab] = narrow


def build_kernel(pairs_ref, *out_refs):
    for w, out_ref in enumerate(out_refs):
        real, imag = pairs_ref[w, 0], pairs_ref[w, 1]
        size = real.shape[0]
        out_ref[:size, :] = jnp.concatenate([real, -imag], axis=1)
        out_ref[size:, :] = jnp.concatenate([imag, real], axis=1)


def energy_at(time, slab, place, core, own_ref, other_ref):
    inner = lax.rem(time, slab)
    group = lax.div(time, slab)
    far = lax.div(group, 2) ^ place
    same = lax.rem(group, 2) == core
    return [
        jnp.where(same, own_ref[peer, far, inner], other_ref[peer, far, inner])
        for peer in range(own_ref.shape[0])
    ]


def choose(time, alive, slab, place, core, own_ref, other_ref, chosen_ref, slot):
    own_rows = own_ref.shape[3]
    for peer, part in enumerate(energy_at(time, slab, place, core, own_ref, other_ref)):
        part = jnp.where(alive, part, jnp.zeros_like(part))
        chosen_ref[slot, peer * own_rows : (peer + 1) * own_rows, :] = part


def signs(lanes):
    return jnp.where(lax.broadcasted_iota(jnp.int32, (1, lanes), 1) < lanes // 2, -1.0, 1.0)


def combined(total):
    rows, lanes = total.shape
    return total[: rows // 2] + signs(lanes) * pltpu.roll(total[rows // 2 :], lanes // 2, 1)


def advance(sum_ref, row_ref, past_refs, columns, inverse_ref, out_ref):
    own_rows, slab, lanes = row_ref.shape
    lanes //= 2
    sign = signs(lanes)
    doubled = [
        jnp.concatenate(
            [c, (sign * pltpu.roll(c.astype(f32), lanes // 2, 1)).astype(bf16)], axis=0
        )
        for c in columns
    ]
    moved = []
    for m in range(2):
        integral = jnp.concatenate(
            [
                sum_ref[pl.ds(m * own_rows + b, slab, stride=2 * own_rows), :]
                for b in range(own_rows)
            ],
            axis=0,
        )
        for past_ref, column in zip(past_refs, doubled):
            past = past_ref[:, :, m * lanes : (m + 1) * lanes].reshape(own_rows * slab, lanes)
            high = past.astype(bf16)
            low = (past - high.astype(f32)).astype(bf16)
            integral += jnp.dot(high, column, preferred_element_type=f32)
            integral += jnp.dot(low, column, preferred_element_type=f32)
        row = row_ref[:, :, m * lanes : (m + 1) * lanes].reshape(own_rows * slab, lanes)
        moved.append(row + step_width * integral)
    moved = lax.dot_general(
        jnp.concatenate(moved, axis=0),
        inverse_ref[...],
        (((1,), (1,)), ((), ())),
        precision=highest,
        preferred_element_type=f32,
    )
    for m in range(2):
        out_ref[:, :, m * lanes : (m + 1) * lanes] = moved[
            m * own_rows * slab : (m + 1) * own_rows * slab
        ].reshape(own_rows, slab, lanes)


def step_kernel(peers, n_past, relative, last, scalar_ref, own_ref, other_ref, row_ref, *rest):
    hist_refs, rest = rest[:peers], rest[peers:]
    past_refs = rest[:n_past]
    inverse_ref, coupling_ref, out_ref = rest[n_past : n_past + 3]
    rest = rest[n_past + 3 :]
    if last:
        chosen_ref, sum_ref = rest
        send_ref = energy_ref = None
    else:
        send_ref, chosen_ref, sum_ref, energy_ref = rest
    slab = row_ref.shape[1]
    slots, orbitals, lanes = chosen_ref.shape
    block = slots // peers
    anchor, home, place, core = [scalar_ref[slots + i] for i in range(4)]
    place = place if relative else 0

    def select(source, slot):
        time = scalar_ref[(source ^ home) * block + slot]
        alive = time <= anchor
        to = source * block + slot
        choose(time, alive, slab, place, core, own_ref, other_ref, chosen_ref, to)

    if slots <= 32:
        for source in range(peers):
            for slot in range(block):
                select(source, slot)
    else:

        @pl.loop(0, peers)
        def _(source):
            for slot in range(block):
                select(source, slot)

    total = None
    for peer in range(peers):
        part = jnp.dot(
            hist_refs[peer][...],
            chosen_ref[peer * block : (peer + 1) * block].reshape(block * orbitals, lanes),
            preferred_element_type=f32,
        )
        total = part if total is None else total + part
    sum_ref[...] = combined(total)
    columns = []
    for past in range(n_past):
        choose(anchor + 1 + past, True, slab, place, core, own_ref, other_ref, chosen_ref, past)
        columns.append(chosen_ref[past])
    advance(sum_ref, row_ref, past_refs, columns, inverse_ref, out_ref)
    if not last:
        send_energy(out_ref, coupling_ref, energy_ref, send_ref)


def spread(block, axis):
    size = lax.axis_size(axis)
    gathered = block[None]
    stride = size // 2
    while stride:
        ring = [(i, i ^ stride) for i in range(size)]
        other = lax.ppermute(gathered, axis, ring)
        gathered = jnp.stack([gathered, other], axis=1).reshape(-1, *block.shape)
        stride //= 2
    return gathered


def body(history, row_now, coupling, step_inverse, start_step, history_time):
    slots_dev, orbitals, slab, parts, lanes = history.shape
    own_rows = row_now.shape[0]
    steps = step_inverse.shape[0]
    peers = lax.axis_size("hist")
    far = lax.axis_size("x")
    groups = slab * parts
    width = lanes // peers
    n_sum = groups * width
    rows = slab * own_rows
    swap = [(0, 1), (1, 0)]
    place = jnp.stack([lax.axis_index(name) for name in ("hist", "x", "c")])
    packed = pl.pallas_call(
        functools.partial(pack_kernel, groups),
        out_shape=[pltpu.VMEM((n_sum, slots_dev * orbitals), bf16)] * peers,
        in_specs=[smem, hbm],
        out_specs=[vmem] * peers,
        scratch_shapes=[
            pltpu.VMEM((slots_dev * orbitals * groups, lanes), bf16),
            pltpu.VMEM((slots_dev * orbitals * groups, lanes), f32),
            pltpu.VMEM((2, peers, width, 128), f32),
            pltpu.SemaphoreType.DMA((slots_dev * orbitals // 128,)),
        ],
        compiler_params=params,
        name="pack",
    )(place, remote(history.reshape(slots_dev * orbitals * groups, lanes)))
    sent = pl.pallas_call(
        first_kernel,
        out_shape=pltpu.VMEM((peers, slab + 1, own_rows, lanes), bf16),
        in_specs=[hbm] * 3,
        out_specs=vmem,
        scratch_shapes=[
            pltpu.VMEM(row_now.shape, f32),
            pltpu.VMEM(coupling.shape, f32),
            pltpu.SMEM((slots_dev,), jnp.int32),
            pltpu.VMEM((rows, lanes), f32),
            pltpu.SemaphoreType.DMA((3,)),
        ],
        compiler_params=params,
        name="first",
    )(remote(row_now), remote(coupling), remote(history_time))
    own = lax.all_to_all(sent, "hist", split_axis=0, concat_axis=0, tiled=True)
    times = own[:, slab, 0, :slots_dev].astype(jnp.int32).reshape(peers * slots_dev)
    scalars = jnp.concatenate([times, start_step, place])
    scalars = pltpu.with_memory_space_constraint(scalars, pltpu.SMEM)
    own = spread(own, "x").swapaxes(0, 1)
    moved = [packed[0]]
    for offset in range(1, peers):
        ring = [(i, i ^ offset) for i in range(peers)]
        moved.append(lax.ppermute(packed[offset], "hist", ring))
    inverse = pl.pallas_call(
        build_kernel,
        out_shape=[pltpu.VMEM((2 * orbitals, 2 * orbitals), f32)] * steps,
        in_specs=[vmem],
        out_specs=[vmem] * steps,
        compiler_params=params,
        name="build",
    )(step_inverse)
    green_shapes = [
        pltpu.VMEM(row_now.shape, f32),
        pltpu.VMEM((peers * far, slab, own_rows, lanes), bf16),
    ]
    green, past = row_now, []
    for w in range(steps):
        last = w == steps - 1
        if w:
            own = lax.all_to_all(sent, ("hist", "x"), split_axis=0, concat_axis=0, tiled=True)
            own = own.reshape(peers, far, slab, own_rows, lanes)
            past.append(green)
        other = lax.ppermute(own, "c", swap)
        outs = [jax.ShapeDtypeStruct(row_now.shape, f32)] if last else green_shapes
        scratch = [
            pltpu.VMEM((peers * slots_dev, orbitals, lanes), bf16),
            pltpu.VMEM((n_sum // 2, lanes), f32),
        ] + [pltpu.VMEM((rows, lanes), f32)] * (not last)
        result = pl.pallas_call(
            functools.partial(step_kernel, peers, len(past), w == 0, last),
            out_shape=outs,
            in_specs=[smem] + [vmem] * (5 + peers + len(past)),
            out_specs=[vmem] * len(outs),
            scratch_shapes=scratch,
            compiler_params=params,
        )(
            scalars,
            local(own),
            local(other),
            local(green),
            *[local(block) for block in moved],
            *[local(row) for row in past],
            local(inverse[w]),
            local(coupling),
        )
        green = result[0]
        if not last:
            sent = result[1]
    return green


def solution(mesh):
    n_hist, n_second = mesh.devices.shape
    split = Mesh(mesh.devices.reshape(n_hist, n_second // 2, 2), ("hist", "x", "c"))
    second = ("x", "c")
    placed = (
        P("hist", None, second, None, None),
        P("hist", second, None),
        P("hist", None),
        P(),
        P(),
        P("hist"),
    )
    return jax.shard_map(
        body, mesh=split, in_specs=placed, out_specs=P("hist", second, None), check_vma=False
    )
```

```python
import functools

import jax
import jax.numpy as jnp
from jax import lax
from jax.experimental import pallas as pl
from jax.experimental.pallas import tpu as pltpu
from jax.sharding import Mesh, PartitionSpec as P


step_width = 0.05
highest = lax.Precision.HIGHEST
bf16 = jnp.bfloat16
f32 = jnp.float32
vmem = pl.BlockSpec(memory_space=pltpu.VMEM)
smem = pl.BlockSpec(memory_space=pltpu.SMEM)
hbm = pl.BlockSpec(memory_space=pltpu.HBM)
params = pltpu.CompilerParams(vmem_limit_bytes=32 * 2**20)


def local(x):
    return pltpu.with_memory_space_constraint(x, pltpu.VMEM)


def remote(x):
    return pltpu.with_memory_space_constraint(x, pltpu.HBM)


def pack_kernel(groups, place_ref, hist_hbm, *rest):
    out_refs, (hist_ref, wide_ref, turned_ref, sems) = rest[:-4], rest[-4:]
    rows = 128 * groups
    width = hist_ref.shape[1] // len(out_refs)
    half = width // 2
    chunks = [pl.ds(c * rows, rows) for c in range(hist_ref.shape[0] // rows)]
    copies = [
        pltpu.make_async_copy(hist_hbm.at[chunk], hist_ref.at[chunk], sems.at[c])
        for c, chunk in enumerate(chunks)
    ]
    for copy in copies:
        copy.start()
    for c, copy in enumerate(copies):
        copy.wait()
        wide_ref[chunks[c], :] = hist_ref[chunks[c], :].astype(f32)
        columns = slice(c * 128, (c + 1) * 128)
        for group in range(groups):
            tile = wide_ref[pl.ds(c * rows + group, 128, stride=groups), :]
            turned = tile.astype(bf16).T.astype(f32)
            for peer in range(len(out_refs)):
                turned_ref[group % 2, peer] = turned[peer * width : (peer + 1) * width]
            for offset, out_ref in enumerate(out_refs):
                for part in range(2):
                    start = (part * groups + group) * half
                    out_ref[start : start + half, columns] = turned_ref[
                        group % 2, place_ref[0] ^ offset, pl.ds(part, half, stride=2), :
                    ].astype(bf16)


def cubic_term(first_real, first_imag, other_real, other_imag):
    square_real = first_real * first_real - first_imag * first_imag
    square_imag = 2.0 * first_real * first_imag
    return (
        square_real * other_real + square_imag * other_imag,
        square_imag * other_real - square_real * other_imag,
    )


def energy_of(lesser, greater, weight_sq):
    half = lesser.shape[-1] // 2
    lr, li = lesser[:, :half], lesser[:, half:]
    gr, gi = greater[:, :half], greater[:, half:]
    less_real, less_imag = cubic_term(lr, li, gr, gi)
    more_real, more_imag = cubic_term(gr, gi, lr, li)
    return jnp.concatenate(
        [weight_sq * (more_real - less_real), weight_sq * (more_imag - less_imag)], axis=-1
    )


def send_energy(row_ref, coupling_ref, scratch_ref, send_ref):
    own_rows, slab, lanes = row_ref.shape
    for b in range(own_rows):
        row = row_ref[b]
        weight = coupling_ref[b : b + 1, :]
        scratch_ref[pl.ds(b, slab, stride=own_rows), :] = energy_of(
            row[:, : lanes // 2], row[:, lanes // 2 :], weight * weight
        )
    for t in range(slab):
        narrow = scratch_ref[t * own_rows : (t + 1) * own_rows, :].astype(bf16)
        for peer in range(send_ref.shape[0]):
            send_ref[peer, t] = narrow


def first_kernel(row_hbm, coupling_hbm, time_hbm, send_ref, row_ref, coupling_ref, time_ref, scratch_ref, sems):
    pairs = ((row_hbm, row_ref), (coupling_hbm, coupling_ref), (time_hbm, time_ref))
    copies = [pltpu.make_async_copy(a, b, sems.at[i]) for i, (a, b) in enumerate(pairs)]
    for copy in copies:
        copy.start()
    for copy in copies:
        copy.wait()
    slab, own_rows, lanes = row_ref.shape[1], row_ref.shape[0], send_ref.shape[3]
    send_energy(row_ref, coupling_ref, scratch_ref, send_ref)
    lane = lax.broadcasted_iota(jnp.int32, (own_rows, lanes), 1)
    times = jnp.zeros((own_rows, lanes), jnp.int32)
    for slot in range(time_ref.shape[0]):
        times = jnp.where(lane == slot, time_ref[slot], times)
    narrow = times.astype(f32).astype(bf16)
    for peer in range(send_ref.shape[0]):
        send_ref[peer, slab] = narrow


def build_kernel(pairs_ref, *out_refs):
    for w, out_ref in enumerate(out_refs):
        real, imag = pairs_ref[w, 0], pairs_ref[w, 1]
        size = real.shape[0]
        out_ref[:size, :] = jnp.concatenate([real, -imag], axis=1)
        out_ref[size:, :] = jnp.concatenate([imag, real], axis=1)


def energy_at(time, slab, place, core, own_ref, other_ref):
    inner = lax.rem(time, slab)
    group = lax.div(time, slab)
    far = lax.div(group, 2) ^ place
    same = lax.rem(group, 2) == core
    return [
        jnp.where(same, own_ref[peer, far, inner], other_ref[peer, far, inner])
        for peer in range(own_ref.shape[0])
    ]


def signs(lanes):
    return jnp.where(lax.broadcasted_iota(jnp.int32, (1, lanes), 1) < lanes // 2, -1.0, 1.0)


def combined(total):
    rows, lanes = total.shape
    return total[: rows // 2] + signs(lanes) * pltpu.roll(total[rows // 2 :], lanes // 2, 1)


def advance(sum_ref, row_ref, past_refs, columns, inverse_ref, out_ref):
    own_rows, slab, lanes = row_ref.shape
    lanes //= 2
    sign = signs(lanes)
    doubled = [
        jnp.concatenate(
            [c, (sign * pltpu.roll(c.astype(f32), lanes // 2, 1)).astype(bf16)], axis=0
        )
        for c in columns
    ]
    moved = []
    for m in range(2):
        integral = jnp.concatenate(
            [
                sum_ref[pl.ds(m * own_rows + b, slab, stride=2 * own_rows), :]
                for b in range(own_rows)
            ],
            axis=0,
        )
        for past_ref, column in zip(past_refs, doubled):
            past = past_ref[:, :, m * lanes : (m + 1) * lanes].reshape(own_rows * slab, lanes)
            high = past.astype(bf16)
            low = (past - high.astype(f32)).astype(bf16)
            integral += jnp.dot(high, column, preferred_element_type=f32)
            integral += jnp.dot(low, column, preferred_element_type=f32)
        row = row_ref[:, :, m * lanes : (m + 1) * lanes].reshape(own_rows * slab, lanes)
        moved.append(row + step_width * integral)
    moved = lax.dot_general(
        jnp.concatenate(moved, axis=0),
        inverse_ref[...],
        (((1,), (1,)), ((), ())),
        precision=highest,
        preferred_element_type=f32,
    )
    for m in range(2):
        out_ref[:, :, m * lanes : (m + 1) * lanes] = moved[
            m * own_rows * slab : (m + 1) * own_rows * slab
        ].reshape(own_rows, slab, lanes)


def step_kernel(peers, n_past, relative, last, scalar_ref, own_ref, other_ref, row_ref, *rest):
    hist_refs, rest = rest[:peers], rest[peers:]
    past_refs = rest[:n_past]
    inverse_ref, coupling_ref, out_ref = rest[n_past : n_past + 3]
    rest = rest[n_past + 3 :]
    if last:
        chosen_ref, sum_ref = rest
        send_ref = energy_ref = None
    else:
        send_ref, chosen_ref, sum_ref, energy_ref = rest
    own_rows, slab = row_ref.shape[:2]
    slots, orbitals, lanes = chosen_ref.shape
    block = slots // peers
    anchor, place, core = [scalar_ref[slots + i] for i in (0, 2, 3)]
    place = place if relative else 0

    def select(far, side, inner):
        time = ((far ^ place) * 2 + (core ^ side)) * slab + inner
        slot = scalar_ref[time]
        alive = time <= anchor
        source_ref = other_ref if side else own_ref
        for peer in range(peers):
            part = source_ref[peer, far, inner]
            chosen_ref[slot, peer * own_rows : (peer + 1) * own_rows, :] = jnp.where(
                alive, part, jnp.zeros_like(part)
            )

    def select_all(inner):
        for far in range(own_ref.shape[1]):
            for side in range(2):
                select(far, side, inner)

    if slots <= 32:
        for inner in range(slab):
            select_all(inner)
    else:
        pl.loop(0, slab)(select_all)

    total = None
    for peer in range(peers):
        part = jnp.dot(
            hist_refs[peer][...],
            chosen_ref[peer * block : (peer + 1) * block].reshape(block * orbitals, lanes),
            preferred_element_type=f32,
        )
        total = part if total is None else total + part
    sum_ref[...] = combined(total)
    columns = []
    for past in range(n_past):
        parts = energy_at(anchor + 1 + past, slab, place, core, own_ref, other_ref)
        for peer, part in enumerate(parts):
            chosen_ref[past, peer * own_rows : (peer + 1) * own_rows, :] = part
        columns.append(chosen_ref[past])
    advance(sum_ref, row_ref, past_refs, columns, inverse_ref, out_ref)
    if not last:
        send_energy(out_ref, coupling_ref, energy_ref, send_ref)


def spread(block, axis):
    size = lax.axis_size(axis)
    gathered = block[None]
    stride = size // 2
    while stride:
        ring = [(i, i ^ stride) for i in range(size)]
        other = lax.ppermute(gathered, axis, ring)
        gathered = jnp.stack([gathered, other], axis=1).reshape(-1, *block.shape)
        stride //= 2
    return gathered


def body(history, row_now, coupling, step_inverse, start_step, history_time):
    slots_dev, orbitals, slab, parts, lanes = history.shape
    own_rows = row_now.shape[0]
    steps = step_inverse.shape[0]
    peers = lax.axis_size("hist")
    far = lax.axis_size("x")
    groups = slab * parts
    width = lanes // peers
    n_sum = groups * width
    rows = slab * own_rows
    swap = [(0, 1), (1, 0)]
    place = jnp.stack([lax.axis_index(name) for name in ("hist", "x", "c")])
    packed = pl.pallas_call(
        functools.partial(pack_kernel, groups),
        out_shape=[pltpu.VMEM((n_sum, slots_dev * orbitals), bf16)] * peers,
        in_specs=[smem, hbm],
        out_specs=[vmem] * peers,
        scratch_shapes=[
            pltpu.VMEM((slots_dev * orbitals * groups, lanes), bf16),
            pltpu.VMEM((slots_dev * orbitals * groups, lanes), f32),
            pltpu.VMEM((2, peers, width, 128), f32),
            pltpu.SemaphoreType.DMA((slots_dev * orbitals // 128,)),
        ],
        compiler_params=params,
        name="pack",
    )(place, remote(history.reshape(slots_dev * orbitals * groups, lanes)))
    sent = pl.pallas_call(
        first_kernel,
        out_shape=pltpu.VMEM((peers, slab + 1, own_rows, lanes), bf16),
        in_specs=[hbm] * 3,
        out_specs=vmem,
        scratch_shapes=[
            pltpu.VMEM(row_now.shape, f32),
            pltpu.VMEM(coupling.shape, f32),
            pltpu.SMEM((slots_dev,), jnp.int32),
            pltpu.VMEM((rows, lanes), f32),
            pltpu.SemaphoreType.DMA((3,)),
        ],
        compiler_params=params,
        name="first",
    )(remote(row_now), remote(coupling), remote(history_time))
    own = lax.all_to_all(sent, "hist", split_axis=0, concat_axis=0, tiled=True)
    times = own[:, slab, 0, :slots_dev].astype(jnp.int32).reshape(peers * slots_dev)
    source = (jnp.arange(peers) ^ place[0])[:, None] * slots_dev + jnp.arange(slots_dev)[None, :]
    found = times[None, :] == jnp.arange(peers * slots_dev)[:, None]
    slot_of = jnp.sum(jnp.where(found, source.reshape(1, -1), 0), axis=1, dtype=jnp.int32)
    scalars = jnp.concatenate([slot_of, start_step, place])
    scalars = pltpu.with_memory_space_constraint(scalars, pltpu.SMEM)
    own = spread(own, "x").swapaxes(0, 1)
    moved = [packed[0]]
    for offset in range(1, peers):
        ring = [(i, i ^ offset) for i in range(peers)]
        moved.append(lax.ppermute(packed[offset], "hist", ring))
    inverse = pl.pallas_call(
        build_kernel,
        out_shape=[pltpu.VMEM((2 * orbitals, 2 * orbitals), f32)] * steps,
        in_specs=[vmem],
        out_specs=[vmem] * steps,
        compiler_params=params,
        name="build",
    )(step_inverse)
    green_shapes = [
        pltpu.VMEM(row_now.shape, f32),
        pltpu.VMEM((peers * far, slab, own_rows, lanes), bf16),
    ]
    green, past = row_now, []
    for w in range(steps):
        last = w == steps - 1
        if w:
            own = lax.all_to_all(sent, ("hist", "x"), split_axis=0, concat_axis=0, tiled=True)
            own = own.reshape(peers, far, slab, own_rows, lanes)
            past.append(green)
        other = lax.ppermute(own, "c", swap)
        outs = [jax.ShapeDtypeStruct(row_now.shape, f32)] if last else green_shapes
        scratch = [
            pltpu.VMEM((peers * slots_dev, orbitals, lanes), bf16),
            pltpu.VMEM((n_sum // 2, lanes), f32),
        ] + [pltpu.VMEM((rows, lanes), f32)] * (not last)
        result = pl.pallas_call(
            functools.partial(step_kernel, peers, len(past), w == 0, last),
            out_shape=outs,
            in_specs=[smem] + [vmem] * (5 + peers + len(past)),
            out_specs=[vmem] * len(outs),
            scratch_shapes=scratch,
            compiler_params=params,
        )(
            scalars,
            local(own),
            local(other),
            local(green),
            *[local(block) for block in moved],
            *[local(row) for row in past],
            local(inverse[w]),
            local(coupling),
        )
        green = result[0]
        if not last:
            sent = result[1]
    return green


def solution(mesh):
    n_hist, n_second = mesh.devices.shape
    split = Mesh(mesh.devices.reshape(n_hist, n_second // 2, 2), ("hist", "x", "c"))
    second = ("x", "c")
    placed = (
        P("hist", None, second, None, None),
        P("hist", second, None),
        P("hist", None),
        P(),
        P(),
        P("hist"),
    )
    return jax.shard_map(
        body, mesh=split, in_specs=placed, out_specs=P("hist", second, None), check_vma=False
    )
```

```python
import functools

import jax
import jax.numpy as jnp
from jax import lax
from jax.experimental import pallas as pl
from jax.experimental.pallas import tpu as pltpu
from jax.sharding import Mesh, PartitionSpec as P


step_width = 0.05
bf16 = jnp.bfloat16
f32 = jnp.float32
vmem = pl.BlockSpec(memory_space=pltpu.VMEM)
smem = pl.BlockSpec(memory_space=pltpu.SMEM)
hbm = pl.BlockSpec(memory_space=pltpu.HBM)
params = pltpu.CompilerParams(vmem_limit_bytes=32 * 2**20)


def local(x):
    return pltpu.with_memory_space_constraint(x, pltpu.VMEM)


def remote(x):
    return pltpu.with_memory_space_constraint(x, pltpu.HBM)


def pack_kernel(groups, place_ref, hist_hbm, *rest):
    out_refs, (hist_ref, wide_ref, turned_ref, sems) = rest[:-4], rest[-4:]
    rows = 128 * groups
    width = hist_ref.shape[1] // len(out_refs)
    half = width // 2
    chunks = [pl.ds(c * rows, rows) for c in range(hist_ref.shape[0] // rows)]
    copies = [
        pltpu.make_async_copy(hist_hbm.at[chunk], hist_ref.at[chunk], sems.at[c])
        for c, chunk in enumerate(chunks)
    ]
    for copy in copies:
        copy.start()
    for c, copy in enumerate(copies):
        copy.wait()
        wide_ref[chunks[c], :] = hist_ref[chunks[c], :].astype(f32)
        columns = slice(c * 128, (c + 1) * 128)
        for group in range(groups):
            tile = wide_ref[pl.ds(c * rows + group, 128, stride=groups), :]
            turned = tile.astype(bf16).T.astype(f32)
            for peer in range(len(out_refs)):
                turned_ref[group % 2, peer] = turned[peer * width : (peer + 1) * width]
            for offset, out_ref in enumerate(out_refs):
                for part in range(2):
                    start = (part * groups + group) * half
                    out_ref[start : start + half, columns] = turned_ref[
                        group % 2, place_ref[0] ^ offset, pl.ds(part, half, stride=2), :
                    ].astype(bf16)


def cubic_term(first_real, first_imag, other_real, other_imag):
    square_real = first_real * first_real - first_imag * first_imag
    square_imag = 2.0 * first_real * first_imag
    return (
        square_real * other_real + square_imag * other_imag,
        square_imag * other_real - square_real * other_imag,
    )


def energy_of(lesser, greater, weight_sq):
    half = lesser.shape[-1] // 2
    lr, li = lesser[:, :half], lesser[:, half:]
    gr, gi = greater[:, :half], greater[:, half:]
    less_real, less_imag = cubic_term(lr, li, gr, gi)
    more_real, more_imag = cubic_term(gr, gi, lr, li)
    return jnp.concatenate(
        [weight_sq * (more_real - less_real), weight_sq * (more_imag - less_imag)], axis=-1
    )


def send_energy(row_ref, coupling_ref, scratch_ref, send_ref):
    own_rows, slab, lanes = row_ref.shape
    for b in range(own_rows):
        row = row_ref[b]
        weight = coupling_ref[b : b + 1, :]
        scratch_ref[pl.ds(b, slab, stride=own_rows), :] = energy_of(
            row[:, : lanes // 2], row[:, lanes // 2 :], weight * weight
        )
    for t in range(slab):
        narrow = scratch_ref[t * own_rows : (t + 1) * own_rows, :].astype(bf16)
        for peer in range(send_ref.shape[0]):
            send_ref[peer, t] = narrow


def first_kernel(row_hbm, coupling_hbm, time_hbm, send_ref, row_ref, coupling_ref, time_ref, scratch_ref, sems):
    pairs = ((row_hbm, row_ref), (coupling_hbm, coupling_ref), (time_hbm, time_ref))
    copies = [pltpu.make_async_copy(a, b, sems.at[i]) for i, (a, b) in enumerate(pairs)]
    for copy in copies:
        copy.start()
    for copy in copies:
        copy.wait()
    slab, own_rows, lanes = row_ref.shape[1], row_ref.shape[0], send_ref.shape[3]
    send_energy(row_ref, coupling_ref, scratch_ref, send_ref)
    lane = lax.broadcasted_iota(jnp.int32, (own_rows, lanes), 1)
    times = jnp.zeros((own_rows, lanes), jnp.int32)
    for slot in range(time_ref.shape[0]):
        times = jnp.where(lane == slot, time_ref[slot], times)
    narrow = times.astype(f32).astype(bf16)
    for peer in range(send_ref.shape[0]):
        send_ref[peer, slab] = narrow


def build_kernel(pairs_ref, *out_refs):
    for w, out_ref in enumerate(out_refs):
        real, imag = pairs_ref[w, 0], pairs_ref[w, 1]
        rows = [jnp.concatenate([real, -imag], axis=1), jnp.concatenate([imag, real], axis=1)]
        turned = jnp.concatenate(rows, axis=0).T
        high = turned.astype(bf16)
        size = turned.shape[0]
        out_ref[:, :size] = high
        out_ref[:, size:] = (turned - high.astype(f32)).astype(bf16)


def energy_at(time, slab, place, core, own_ref, other_ref):
    inner = lax.rem(time, slab)
    group = lax.div(time, slab)
    far = lax.div(group, 2) ^ place
    same = lax.rem(group, 2) == core
    return [
        jnp.where(same, own_ref[peer, far, inner], other_ref[peer, far, inner])
        for peer in range(own_ref.shape[0])
    ]


def signs(lanes):
    return jnp.where(lax.broadcasted_iota(jnp.int32, (1, lanes), 1) < lanes // 2, -1.0, 1.0)


def combined(total):
    rows, lanes = total.shape
    return total[: rows // 2] + signs(lanes) * pltpu.roll(total[rows // 2 :], lanes // 2, 1)


def advance(sum_ref, row_ref, past_refs, columns, inverse_ref, out_ref):
    own_rows, slab, lanes = row_ref.shape
    lanes //= 2
    sign = signs(lanes)
    doubled = [
        jnp.concatenate(
            [c, (sign * pltpu.roll(c.astype(f32), lanes // 2, 1)).astype(bf16)], axis=0
        )
        for c in columns
    ]
    moved = []
    for m in range(2):
        integral = jnp.concatenate(
            [
                sum_ref[pl.ds(m * own_rows + b, slab, stride=2 * own_rows), :]
                for b in range(own_rows)
            ],
            axis=0,
        )
        for past_ref, column in zip(past_refs, doubled):
            past = past_ref[:, :, m * lanes : (m + 1) * lanes].reshape(own_rows * slab, lanes)
            high = past.astype(bf16)
            low = (past - high.astype(f32)).astype(bf16)
            integral += jnp.dot(high, column, preferred_element_type=f32)
            integral += jnp.dot(low, column, preferred_element_type=f32)
        row = row_ref[:, :, m * lanes : (m + 1) * lanes].reshape(own_rows * slab, lanes)
        moved.append(row + step_width * integral)
    moved = jnp.concatenate(moved, axis=0)
    high = moved.astype(bf16)
    low = (moved - high.astype(f32)).astype(bf16)
    both = jnp.dot(high, inverse_ref[...], preferred_element_type=f32)
    rest = jnp.dot(low, inverse_ref[:, :lanes], preferred_element_type=f32)
    moved = both[:, :lanes] + (both[:, lanes:] + rest)
    for m in range(2):
        out_ref[:, :, m * lanes : (m + 1) * lanes] = moved[
            m * own_rows * slab : (m + 1) * own_rows * slab
        ].reshape(own_rows, slab, lanes)


def step_kernel(peers, n_past, relative, last, scalar_ref, own_ref, other_ref, row_ref, *rest):
    hist_refs, rest = rest[:peers], rest[peers:]
    past_refs = rest[:n_past]
    inverse_ref, coupling_ref, out_ref = rest[n_past : n_past + 3]
    rest = rest[n_past + 3 :]
    if last:
        chosen_ref, sum_ref = rest
        send_ref = energy_ref = None
    else:
        send_ref, chosen_ref, sum_ref, energy_ref = rest
    own_rows, slab = row_ref.shape[:2]
    slots, orbitals, lanes = chosen_ref.shape
    block = slots // peers
    anchor, place, core = [scalar_ref[slots + i] for i in (0, 2, 3)]
    place = place if relative else 0

    def select(source, slot):
        time = scalar_ref[source * block + slot]
        alive = time <= anchor
        parts = energy_at(time, slab, place, core, own_ref, other_ref)
        for peer, part in enumerate(parts):
            chosen_ref[
                source * block + slot, peer * own_rows : (peer + 1) * own_rows, :
            ] = jnp.where(alive, part, jnp.zeros_like(part))

    if slots > 32:

        @pl.loop(0, peers)
        def _(source):
            for slot in range(block):
                select(source, slot)

    total = None
    for peer in range(peers):
        if slots <= 32:
            for slot in range(block):
                select(peer, slot)
        part = jnp.dot(
            hist_refs[peer][...],
            chosen_ref[peer * block : (peer + 1) * block].reshape(block * orbitals, lanes),
            preferred_element_type=f32,
        )
        total = part if total is None else total + part
    sum_ref[...] = combined(total)
    columns = []
    for past in range(n_past):
        parts = energy_at(anchor + 1 + past, slab, place, core, own_ref, other_ref)
        for peer, part in enumerate(parts):
            chosen_ref[past, peer * own_rows : (peer + 1) * own_rows, :] = part
        columns.append(chosen_ref[past])
    advance(sum_ref, row_ref, past_refs, columns, inverse_ref, out_ref)
    if not last:
        send_energy(out_ref, coupling_ref, energy_ref, send_ref)


def spread(block, axis):
    size = lax.axis_size(axis)
    gathered = block[None]
    stride = size // 2
    while stride:
        ring = [(i, i ^ stride) for i in range(size)]
        other = lax.ppermute(gathered, axis, ring)
        gathered = jnp.stack([gathered, other], axis=1).reshape(-1, *block.shape)
        stride //= 2
    return gathered


def body(history, row_now, coupling, step_inverse, start_step, history_time):
    slots_dev, orbitals, slab, parts, lanes = history.shape
    own_rows = row_now.shape[0]
    steps = step_inverse.shape[0]
    peers = lax.axis_size("hist")
    far = lax.axis_size("x")
    groups = slab * parts
    width = lanes // peers
    n_sum = groups * width
    rows = slab * own_rows
    swap = [(0, 1), (1, 0)]
    place = jnp.stack([lax.axis_index(name) for name in ("hist", "x", "c")])
    packed = pl.pallas_call(
        functools.partial(pack_kernel, groups),
        out_shape=[pltpu.VMEM((n_sum, slots_dev * orbitals), bf16)] * peers,
        in_specs=[smem, hbm],
        out_specs=[vmem] * peers,
        scratch_shapes=[
            pltpu.VMEM((slots_dev * orbitals * groups, lanes), bf16),
            pltpu.VMEM((slots_dev * orbitals * groups, lanes), f32),
            pltpu.VMEM((2, peers, width, 128), f32),
            pltpu.SemaphoreType.DMA((slots_dev * orbitals // 128,)),
        ],
        compiler_params=params,
        name="pack",
    )(place, remote(history.reshape(slots_dev * orbitals * groups, lanes)))
    sent = pl.pallas_call(
        first_kernel,
        out_shape=pltpu.VMEM((peers, slab + 1, own_rows, lanes), bf16),
        in_specs=[hbm] * 3,
        out_specs=vmem,
        scratch_shapes=[
            pltpu.VMEM(row_now.shape, f32),
            pltpu.VMEM(coupling.shape, f32),
            pltpu.SMEM((slots_dev,), jnp.int32),
            pltpu.VMEM((rows, lanes), f32),
            pltpu.SemaphoreType.DMA((3,)),
        ],
        compiler_params=params,
        name="first",
    )(remote(row_now), remote(coupling), remote(history_time))
    own = lax.all_to_all(sent, "hist", split_axis=0, concat_axis=0, tiled=True)
    times = own[:, slab, 0, :slots_dev].astype(jnp.int32).reshape(peers * slots_dev)
    nearest = jnp.take(times.reshape(peers, slots_dev), jnp.arange(peers) ^ place[0], axis=0)
    scalars = jnp.concatenate([nearest.reshape(-1), start_step, place])
    scalars = pltpu.with_memory_space_constraint(scalars, pltpu.SMEM)
    own = spread(own, "x").swapaxes(0, 1)
    moved = [packed[0]]
    for offset in range(1, peers):
        ring = [(i, i ^ offset) for i in range(peers)]
        moved.append(lax.ppermute(packed[offset], "hist", ring))
    inverse = pl.pallas_call(
        build_kernel,
        out_shape=[pltpu.VMEM((2 * orbitals, 4 * orbitals), bf16)] * steps,
        in_specs=[vmem],
        out_specs=[vmem] * steps,
        compiler_params=params,
        name="build",
    )(step_inverse)
    green_shapes = [
        pltpu.VMEM(row_now.shape, f32),
        pltpu.VMEM((peers * far, slab, own_rows, lanes), bf16),
    ]
    green, past = row_now, []
    for w in range(steps):
        last = w == steps - 1
        if w:
            own = lax.all_to_all(sent, ("hist", "x"), split_axis=0, concat_axis=0, tiled=True)
            own = own.reshape(peers, far, slab, own_rows, lanes)
            past.append(green)
        other = lax.ppermute(own, "c", swap)
        outs = [jax.ShapeDtypeStruct(row_now.shape, f32)] if last else green_shapes
        scratch = [
            pltpu.VMEM((peers * slots_dev, orbitals, lanes), bf16),
            pltpu.VMEM((n_sum // 2, lanes), f32),
        ] + [pltpu.VMEM((rows, lanes), f32)] * (not last)
        result = pl.pallas_call(
            functools.partial(step_kernel, peers, len(past), w == 0, last),
            out_shape=outs,
            in_specs=[smem] + [vmem] * (5 + peers + len(past)),
            out_specs=[vmem] * len(outs),
            scratch_shapes=scratch,
            compiler_params=params,
        )(
            scalars,
            local(own),
            local(other),
            local(green),
            *[local(block) for block in moved],
            *[local(row) for row in past],
            local(inverse[w]),
            local(coupling),
        )
        green = result[0]
        if not last:
            sent = result[1]
    return green


def solution(mesh):
    n_hist, n_second = mesh.devices.shape
    split = Mesh(mesh.devices.reshape(n_hist, n_second // 2, 2), ("hist", "x", "c"))
    second = ("x", "c")
    placed = (
        P("hist", None, second, None, None),
        P("hist", second, None),
        P("hist", None),
        P(),
        P(),
        P("hist"),
    )
    return jax.shard_map(
        body, mesh=split, in_specs=placed, out_specs=P("hist", second, None), check_vma=False
    )
```
